32 devices in a mesh: ctx: 8 (over y, x, core), fsdp: 4 (over z).
Axes of the slice: x: 2, y: 2, z: 4, core: 2. Of those that a mesh axis runs over, the one named last changes fastest.
Arguments:
- hidden_in: bfloat16 [4, 1024, 2048], P('fsdp', 'ctx'), may hold values from -6 to 6
- cotangent: bfloat16 [4, 1024, 2048], P('fsdp', 'ctx'), may hold values from -6 to 6
- doc_ids: int32 [4, 1024], P('fsdp'), may hold values from 0 to 3, never falling along the last dimension, each value on 1 to 512 neighbouring positions
- pair_index: int32 [8], replicated, may hold values from 0 to 7, each once
- w_query: bfloat16 [2048, 2048], P('fsdp'), may hold values from -0.125 to 0.125
- w_key: bfloat16 [256, 2048], P('fsdp'), may hold values from -0.125 to 0.125
- w_value: bfloat16 [256, 2048], P('fsdp'), may hold values from -0.125 to 0.125
- w_out: bfloat16 [2048, 2048], P('fsdp'), may hold values from -0.5 to 0.5
- w_gate: bfloat16 [5632, 2048], P('fsdp'), may hold values from -0.125 to 0.125
- w_up: bfloat16 [5632, 2048], P('fsdp'), may hold values from -0.125 to 0.125
- w_down: bfloat16 [5632, 2048], P('fsdp'), may hold values from -0.078125 to 0.078125
- norm_attn: bfloat16 [2048], replicated, may hold values from 0.5 to 1.5
- norm_ffn: bfloat16 [2048], replicated, may hold values from 0.5 to 1.5
Outputs:
- hidden_out: bfloat16 [4, 1024, 2048], P('fsdp', 'ctx')
- grad_hidden: bfloat16 [4, 1024, 2048], P('fsdp', 'ctx')
- grad_w_query: float32 [2048, 2048], P('fsdp')
- grad_w_key: float32 [256, 2048], P('fsdp')
- grad_w_value: float32 [256, 2048], P('fsdp')
- grad_w_out: float32 [2048, 2048], P('fsdp')
- grad_w_gate: float32 [5632, 2048], P('fsdp')
- grad_w_up: float32 [5632, 2048], P('fsdp')
- grad_w_down: float32 [5632, 2048], P('fsdp')
- grad_norm_attn: float32 [2048], replicated
- grad_norm_ffn: float32 [2048], replicated
The draws below stay inside these ranges and needn't reach their ends.
Inputs may be any that keep to these rules, and one draw needn't show every extreme that they name: doc_ids never falls along a sequence; each document holds 1 to 512 tokens and one exactly 512. A permutation; ctx index c holds causal blocks pair_index[c] and 15 - pair_index[c] of its sequence.
All inputs are finite; a program needn't handle non-finite values.
Results may differ from the reference program's by a relative error of at most 0.023.
Values may be sent and summed in bfloat16 or wider, within the bound.
No kernel may reach another device: no remote copies, remote signals or barrier semaphores. Data moves between devices by JAX's collectives and lax.ppermute only.
A program may use at most 768 MiB of HBM per device.

```python
import math
import jax
import jax.numpy as jnp
import numpy as np
from jax import lax

D = 2048
H = 32
KV = 4
HD = 64
FF = 5632
TOK_DEV = 128
DOCS = 4
SEQS = 4
L = 1024
N_CTX = 8


def levels(rng, extent, cuts, least, largest):
    loudness, own = 1.0, jax.random.fold_in(rng, 6)
    for dim, parts in cuts:
        draws = jnp.exp(jax.random.uniform(jax.random.fold_in(own, dim), (parts,), jnp.float32, least / len(cuts), largest / len(cuts)))
        loudness = loudness * jnp.repeat(draws, extent[dim] // parts).reshape([-1 if axis == dim else 1 for axis in range(len(extent))])
    return loudness


def profile(number_of, total, most, slope):
    loads = [(1 << 20) // math.isqrt(rank ** slope) + 1 for rank in range(2, number_of + 1)]
    surplus, counts = total - most - (number_of - 1), [1] * (number_of - 1)
    while surplus > 0:
        movable = [i for i in range(number_of - 1) if counts[i] < most]
        mass, left = sum([loads[i] for i in movable]), surplus
        for i in movable:
            extra = min(most - counts[i], max(1, left * loads[i] // mass), surplus)
            counts[i] = counts[i] + extra
            surplus = surplus - extra
    return np.array([most] + counts)


def uneven(rng, amount, total, most, skew):
    if amount == 2:
        one = jax.random.randint(rng, (), max(1, total - most), min(most, total - 1) + 1)
        return jnp.stack([one, total - one])
    tallies = jnp.asarray(profile(amount, total, most, skew), jnp.int32)
    couples = (amount - 1) // 2
    donor, sink = tallies[1:1 + 2 * couples:2], tallies[2:2 + 2 * couples:2]
    slack = jnp.minimum(donor - 1, most - sink)
    moved = jax.random.randint(jax.random.fold_in(rng, 1), (couples,), 0, 1 << 20) % (slack + 1)
    tallies = tallies.at[1:1 + 2 * couples:2].set(donor - moved).at[2:2 + 2 * couples:2].set(sink + moved)
    return tallies[jax.random.permutation(jax.random.fold_in(rng, 2), amount)]


def centred(key, shape, width, most, split=(), kind=jnp.bfloat16):
    drawn = width * jax.random.normal(key, shape, jnp.float32)
    if split:
        drawn = drawn * levels(key, shape, split, -0.22, 0.18)
    return jnp.clip(drawn, -most, most).astype(kind)


def setup_inputs(seed: int = 0) -> dict:
    streams_of = jax.random.split(jax.random.key(seed), 14)
    return {
        "hidden_in": centred(streams_of[0], (SEQS, L, D), 1.0, 6.0, ((0, 4), (1, 8))),
        "cotangent": centred(streams_of[1], (SEQS, L, D), 1.0, 6.0, ((0, 4), (1, 8))),
        "doc_ids": jax.vmap(lambda own: jnp.searchsorted(jnp.cumsum(uneven(own, DOCS, L, L // 2, 0)), jnp.arange(L), side="right"))(jax.random.split(streams_of[2], SEQS)).reshape((SEQS, L)).astype(jnp.int32),
        "pair_index": jax.random.permutation(streams_of[3], N_CTX).astype(jnp.int32),
        "w_query": centred(streams_of[4], (H * HD, D), D ** -0.5, 0.125, ((0, 4),)),
        "w_key": centred(streams_of[5], (KV * HD, D), D ** -0.5, 0.125, ((0, 4),)),
        "w_value": centred(streams_of[6], (KV * HD, D), D ** -0.5, 0.125, ((0, 4),)),
        "w_out": centred(streams_of[7], (D, H * HD), (H * HD // 16) ** -0.5, 0.5, ((0, 4),)),
        "w_gate": centred(streams_of[8], (FF, D), D ** -0.5, 0.125, ((0, 4),)),
        "w_up": centred(streams_of[9], (FF, D), D ** -0.5, 0.125, ((0, 4),)),
        "w_down": centred(streams_of[10], (FF, D), FF ** -0.5, 0.078125, ((0, 4),)),
        "norm_attn": jnp.clip(1.0 + 0.1 * jax.random.normal(streams_of[11], (D,), jnp.float32), 0.5, 1.5).astype(jnp.bfloat16),
        "norm_ffn": jnp.clip(1.0 + 0.1 * jax.random.normal(streams_of[12], (D,), jnp.float32), 0.5, 1.5).astype(jnp.bfloat16),
    }


@jax.custom_vjp
def low(v):
    return lax.optimization_barrier(v.astype(jnp.bfloat16)).astype(jnp.float32)

@jax.custom_vjp
def low_back(v):
    return v

def low_keep(v):
    return (low(v), None)

def low_pass(kept, grad):
    return (grad,)

def back_keep(v):
    return (v, None)

def back_low(kept, grad):
    return (low(grad),)
low.defvjp(low_keep, low_pass)
low_back.defvjp(back_keep, back_low)
EPSILON = 1e-05
MASKED = -1e+30
HIGHEST = lax.Precision.HIGHEST

def matmul_t(left_side, right_side):
    return jnp.dot(left_side, right_side.T, precision=HIGHEST, preferred_element_type=jnp.float32)

def rms_scale(values, gain_vec):
    return values * lax.rsqrt(lax.optimization_barrier(jnp.mean(values * values, axis=-1, keepdims=True)) + EPSILON) * gain_vec

def rotary(values, angles):
    middle = values.shape[-1] // 2
    cosine = jnp.cos(angles)[:, None, :]
    sine_part = jnp.sin(angles)[:, None, :]
    lower_half = values[..., :middle]
    upper_half = values[..., middle:]
    return jnp.concatenate([lower_half * cosine - upper_half * sine_part, upper_half * cosine + lower_half * sine_part], axis=-1)

def dealt_positions(pair_index):
    block_rows = TOK_DEV // 2
    row_ids = jnp.arange(TOK_DEV * N_CTX, dtype=jnp.int32)
    paired = jnp.take(pair_index, row_ids // TOK_DEV).astype(jnp.int32)
    causal_block = jnp.where(row_ids // block_rows % 2 == 0, paired, 2 * N_CTX - 1 - paired)
    return (causal_block * block_rows + row_ids % block_rows).astype(jnp.int32)

def attend(query_rot, key_rot, value_rows, positions, segments):
    length = query_rot.shape[0]
    query_block = math.gcd(length, 512)
    block_count = length // query_block
    scale_factor = HD ** (-0.5)

    def one_block(block_args):
        queries, query_pos, query_seg = block_args
        raw_scores = low_back(jnp.einsum('tkgd,skd->tkgs', queries, key_rot, precision=HIGHEST))
        allowed = (positions[None, :] <= query_pos[:, None]) & (segments[None, :] == query_seg[:, None])
        scores = jnp.where(allowed[:, None, None, :], raw_scores * scale_factor, MASKED)
        softmax_w = low(jax.nn.softmax(scores, axis=-1))
        return jnp.einsum('tkgs,skd->tkgd', softmax_w, value_rows, precision=HIGHEST)
    blocks = lax.map(jax.checkpoint(one_block), (query_rot.reshape(block_count, query_block, KV, H // KV, HD), positions.reshape(block_count, query_block), segments.reshape(block_count, query_block)))
    return blocks.reshape(length, KV, H // KV, HD)

def layer_forward(hidden, weights, doc_ids, positions):
    w_query, w_key, w_value, w_out, w_gate, w_up, w_down, norm_attn, norm_ffn = weights
    length = positions.shape[0]
    frequency = jnp.exp(jnp.arange(HD // 2, dtype=jnp.float32) * (-2.0 * math.log(10000.0) / HD))
    angles = positions.astype(jnp.float32)[:, None] * frequency[None, :]

    def one_sequence(inputs):
        seq_rows, doc_row = inputs
        segments = jnp.take(doc_row, positions)
        normed = low(rms_scale(seq_rows, norm_attn))
        query_pre = low_back(matmul_t(normed, w_query)).reshape(length, H, HD)
        key_pre = low_back(matmul_t(normed, w_key)).reshape(length, KV, HD)
        value_rows = low(low_back(matmul_t(normed, w_value))).reshape(length, KV, HD)
        query_rot = low(rotary(query_pre, angles)).reshape(length, KV, H // KV, HD)
        key_rot = low(rotary(key_pre, angles))
        attended = attend(query_rot, key_rot, value_rows, positions, segments).reshape(length, H * HD)
        mixed_rows = low(low_back(attended))
        residual = seq_rows + low_back(matmul_t(mixed_rows, w_out))
        normed_ffn = low(rms_scale(residual, norm_ffn))
        gate_proj = low_back(matmul_t(normed_ffn, w_gate))
        up_proj = low_back(matmul_t(normed_ffn, w_up))
        hidden_units = low(jax.nn.silu(gate_proj) * up_proj)
        return residual + jnp.dot(hidden_units, w_down, precision=HIGHEST, preferred_element_type=jnp.float32)
    return lax.map(jax.checkpoint(one_sequence), (hidden, doc_ids))

def reference(hidden_in, cotangent, doc_ids, pair_index, w_query, w_key, w_value, w_out, w_gate, w_up, w_down, norm_attn, norm_ffn):
    positions = dealt_positions(pair_index)
    params = tuple((tensor.astype(jnp.float32) for tensor in (w_query, w_key, w_value, w_out, w_gate, w_up, w_down, norm_attn, norm_ffn)))

    def forward(hidden, weights):
        return layer_forward(hidden, weights, doc_ids, positions)
    output, pullback = jax.vjp(forward, hidden_in.astype(jnp.float32), params)
    grad_input, grad_params = pullback(cotangent.astype(jnp.float32))
    return (output.astype(jnp.bfloat16), grad_input.astype(jnp.bfloat16), grad_params[0], grad_params[1], grad_params[2], grad_params[3], grad_params[4], grad_params[5], grad_params[6], grad_params[7], grad_params[8])
```

```python
import math

import jax
import jax.numpy as jnp
from jax import lax
from jax.experimental import pallas as pl
from jax.experimental.pallas import tpu as pltpu
from jax.sharding import PartitionSpec as P

H = 32
KV = 4
HD = 64
LANES = 2 * HD

EPSILON = 1e-05
MASKED = -1e30


bf16 = jnp.bfloat16
f32 = jnp.float32


def product_t(a, b):
    return lax.dot_general(a, b, (((1,), (1,)), ((), ())), preferred_element_type=f32)


def product_n(a, b):
    return lax.dot_general(a, b, (((1,), (0,)), ((), ())), preferred_element_type=f32)


def product_tn(a, b):
    return lax.dot_general(a, b, (((0,), (0,)), ((), ())), preferred_element_type=f32)


def rows_at(x, start, size, axis=0):
    return lax.dynamic_slice_in_dim(x, start, size, axis)


def swap(x, axis, mask):
    n = lax.axis_size(axis)
    return lax.ppermute(x, axis, [(i, i ^ mask) for i in range(n)])


def gather_z(x):
    n = lax.axis_size("fsdp")
    if n != 4:
        return [x] + [swap(x, "fsdp", r) for r in range(1, n)]
    f = lax.axis_index("fsdp")
    two = swap(x, "fsdp", 2)
    one = swap(x, "fsdp", 1)
    near = lax.ppermute(x, "fsdp", [(1, 2), (2, 1)])
    far = lax.ppermute(two, "fsdp", [(2, 3), (1, 0)])
    inner = (f == 1) | (f == 2)
    return [x, one, two, jnp.where(inner, near, far)]


def scatter_z(parts):
    n = lax.axis_size("fsdp")
    if n != 4:
        got = [swap(parts[r], "fsdp", r) for r in range(1, n)]
        return sum([g.astype(f32) for g in got], parts[0].astype(f32))
    far = lax.ppermute(parts[3], "fsdp", [(3, 2), (0, 1)])
    one = swap(parts[1], "fsdp", 1)
    near = lax.ppermute(parts[3], "fsdp", [(1, 2), (2, 1)])
    two = swap((parts[2].astype(f32) + far.astype(f32)).astype(bf16), "fsdp", 2)
    return parts[0].astype(f32) + one.astype(f32) + near.astype(f32) + two.astype(f32)


def exchange_z(blocks):
    return [blocks[0]] + [swap(blocks[r], "fsdp", r) for r in range(1, len(blocks))]


def gather_ctx(x):
    n = lax.axis_size("ctx")
    own = jnp.stack([x] + [swap(x, "ctx", r) for r in range(2, n, 2)])
    other = swap(own, "ctx", 1)
    return jnp.stack([own, other], 1).reshape((n,) + x.shape)


def scatter_ctx(x):
    n = lax.axis_size("ctx")
    pairs = x.reshape((n // 2, 2) + x.shape[1:])
    got = swap(pairs[:, 1], "ctx", 1)
    both = (pairs[:, 0].astype(f32) + got.astype(f32)).astype(bf16)
    return [both[0]] + [swap(both[r], "ctx", 2 * r) for r in range(1, n // 2)]


def bit_of(index, mask):
    return (index // mask) % 2


def place_kernel(where_ref, mine_ref, theirs_ref, out_ref):
    step = pl.program_id(0)
    half = pl.num_programs(0) // 2

    @pl.when(step < half)
    def _():
        out_ref[...] = mine_ref[...].astype(out_ref.dtype)

    @pl.when(step >= half)
    def _():
        out_ref[...] = theirs_ref[...].astype(out_ref.dtype)


def place(mine, theirs, where, dtype):
    count = where.shape[0]
    half = count // 2
    rows, cols = mine.shape[0] // half, mine.shape[1]
    out = pl.pallas_call(
        place_kernel,
        out_shape=jax.ShapeDtypeStruct((count, rows, cols), dtype),
        grid_spec=pltpu.PrefetchScalarGridSpec(
            num_scalar_prefetch=1,
            grid=(count,),
            in_specs=[
                pl.BlockSpec((1, rows, cols), lambda i, w: (jnp.minimum(i, half - 1), 0, 0)),
                pl.BlockSpec((1, rows, cols), lambda i, w: (jnp.maximum(i - half, 0), 0, 0)),
            ],
            out_specs=pl.BlockSpec((1, rows, cols), lambda i, w: (w[i], 0, 0)),
        ),
        name="place",
    )(where, mine.reshape(half, rows, cols), theirs.reshape(half, rows, cols))
    return out.reshape(count * rows, cols)


def grad_sum(left, right, masks):
    me = lax.axis_index("ctx")
    total = left.shape[1]
    width = total // 2
    bit = bit_of(me, masks[0])
    keep = bit * width
    sent = product_tn(rows_at(left, (1 - bit) * width, width, 1), right).astype(bf16)
    got = swap(sent, "ctx", masks[0])
    width //= 2
    bit = bit_of(me, masks[1])
    away, home = (1 - bit) * width, bit * width
    sent = product_tn(rows_at(left, keep + away, width, 1), right) + rows_at(got, away, width).astype(f32)
    got_two = swap(sent.astype(bf16), "ctx", masks[1])
    kept = product_tn(rows_at(left, keep + home, width, 1), right) + rows_at(got, home, width).astype(f32)
    kept = lax.optimization_barrier(kept.astype(bf16)).astype(f32) + got_two.astype(f32)
    for mask in masks[2:]:
        width //= 2
        bit = bit_of(me, mask)
        got = swap(rows_at(kept, (1 - bit) * width, width).astype(bf16), "ctx", mask)
        kept = rows_at(kept, bit * width, width) + got.astype(f32)
    piece = kept.astype(bf16)
    for mask in masks[:0:-1]:
        piece = jnp.concatenate([piece, swap(piece, "ctx", mask)], 0)
    other = swap(piece, "ctx", masks[0])
    count = 1 << len(masks)
    slots = jnp.arange(count, dtype=jnp.int32)
    where = jnp.zeros((count,), jnp.int32)
    for level, mask in enumerate(masks):
        weight = count >> (level + 1)
        where = where + weight * ((slots // weight + bit_of(me, mask)) % 2)
    return place(piece, other, where, f32)


def turned(x, cosine, sine):
    lane = lax.broadcasted_iota(jnp.int32, x.shape, 1) % HD
    partner = jnp.where(
        lane < HD // 2, pltpu.roll(x, LANES - HD // 2, 1), pltpu.roll(x, HD // 2, 1)
    )
    return x * cosine + partner * sine


def rotate_kernel(x_ref, cos_ref, sin_ref, q_ref, kv_ref):
    cosine, sine = cos_ref[...], sin_ref[...]
    wide = q_ref.shape[-1]
    for at in range(0, wide, LANES):
        x = turned(x_ref[0, :, at : at + LANES], cosine, sine)
        q_ref[0, :, at : at + LANES] = (x * HD**-0.5).astype(bf16)
    x = x_ref[0, :, wide : wide + LANES]
    lane = lax.broadcasted_iota(jnp.int32, x.shape, 1)
    kv_ref[0] = jnp.where(lane < HD, turned(x, cosine, sine), x).astype(bf16)


def rotate(x, cosine, sine):
    slots, rows, width = x.shape
    wide = width - LANES
    return pl.pallas_call(
        rotate_kernel,
        out_shape=(
            jax.ShapeDtypeStruct((slots, rows, wide), bf16),
            jax.ShapeDtypeStruct((slots, rows, LANES), bf16),
        ),
        grid=(slots,),
        in_specs=[
            pl.BlockSpec((1, rows, width), lambda i: (i, 0, 0)),
            pl.BlockSpec((rows, LANES), lambda i: (0, 0)),
            pl.BlockSpec((rows, LANES), lambda i: (0, 0)),
        ],
        out_specs=(
            pl.BlockSpec((1, rows, wide), lambda i: (i, 0, 0)),
            pl.BlockSpec((1, rows, LANES), lambda i: (i, 0, 0)),
        ),
        name="rotate",
    )(x, cosine, sine)


def low_half(x):
    lane = lax.broadcasted_iota(jnp.int32, x.shape, 1)
    return jnp.concatenate(
        [jnp.where(lane < HD, x, 0.0), jnp.where(lane < HD, pltpu.roll(x, HD, 1), 0.0)], 0
    )


def high_half(x):
    lane = lax.broadcasted_iota(jnp.int32, x.shape, 1)
    return jnp.concatenate(
        [jnp.where(lane < HD, 0.0, pltpu.roll(x, HD, 1)), jnp.where(lane < HD, 0.0, x)], 0
    )


def join_high(x):
    rows = x.shape[0] // 2
    lane = lax.broadcasted_iota(jnp.int32, (rows, LANES), 1)
    return jnp.where(lane < HD, pltpu.roll(x[:rows], HD, 1), x[rows:])


def join_low(x):
    rows = x.shape[0] // 2
    lane = lax.broadcasted_iota(jnp.int32, (rows, LANES), 1)
    return jnp.where(lane < HD, x[:rows], pltpu.roll(x[rows:], HD, 1))


def bias_of(qpos_ref, qstart_ref, kpos_ref):
    key = kpos_ref[...]
    return jnp.where((key <= qpos_ref[...]) & (key >= qstart_ref[0]), 0.0, MASKED)


def attend_kernel(q_ref, kv_ref, qpos_ref, qstart_ref, kpos_ref, mixed_ref, aux_ref):
    rows = q_ref.shape[1]
    kv = kv_ref[...].reshape(-1, LANES)
    bias = bias_of(qpos_ref, qstart_ref, kpos_ref)
    bias = jnp.concatenate([bias, bias], 0)
    for pair in range(q_ref.shape[2] // LANES):
        x = q_ref[0, :, pair * LANES : (pair + 1) * LANES].astype(f32)
        scores = product_t(low_half(x).astype(bf16), kv) + bias
        top = jnp.max(scores, -1, keepdims=True)
        weights = jnp.exp(scores - top)
        total = jnp.sum(weights, -1, keepdims=True)
        out = product_n(weights.astype(bf16), kv) / total
        lane = lax.broadcasted_iota(jnp.int32, out.shape, 1)
        aux = jnp.where(lane < HD, top + jnp.log(total), out)
        aux_ref[0, 2 * pair] = aux[:rows]
        aux_ref[0, 2 * pair + 1] = aux[rows:]
        mixed_ref[0, :, pair * LANES : (pair + 1) * LANES] = join_high(out).astype(bf16)


def attend_specs(slots, groups, rows, wide):
    return [
        pl.BlockSpec((1, rows, wide), lambda i: (i, 0, 0)),
        pl.BlockSpec((groups, 1, rows, LANES), lambda i: (0, i, 0, 0)),
        pl.BlockSpec((rows, 1), lambda i: (0, 0)),
        pl.BlockSpec((1, rows, 1), lambda i: (i, 0, 0)),
        pl.BlockSpec((1, groups * rows), lambda i: (0, 0)),
    ]


def attend(q, kv, qpos, qstart, kpos):
    slots, rows, wide = q.shape
    groups = kv.shape[0]
    heads = wide // HD
    return pl.pallas_call(
        attend_kernel,
        out_shape=(
            jax.ShapeDtypeStruct((slots, rows, wide), bf16),
            jax.ShapeDtypeStruct((slots, heads, rows, LANES), f32),
        ),
        grid=(slots,),
        in_specs=attend_specs(slots, groups, rows, wide),
        out_specs=(
            pl.BlockSpec((1, rows, wide), lambda i: (i, 0, 0)),
            pl.BlockSpec((1, heads, rows, LANES), lambda i: (i, 0, 0, 0)),
        ),
        name="attend",
    )(q, kv, qpos, qstart, kpos)


def attend_back_kernel(
    q_ref, kv_ref, qpos_ref, qstart_ref, kpos_ref, aux_ref, grad_ref, cos_ref, sin_ref, gq_ref, gkv_ref
):
    kv = kv_ref[...].reshape(-1, LANES)
    bias = bias_of(qpos_ref, qstart_ref, kpos_ref)
    bias = jnp.concatenate([bias, bias], 0)
    cosine, sine = cos_ref[...], sin_ref[...]
    total = jnp.zeros(kv.shape, f32)
    for pair in range(q_ref.shape[2] // LANES):
        cols = slice(pair * LANES, (pair + 1) * LANES)
        q = low_half(q_ref[0, :, cols].astype(f32)).astype(bf16)
        grad = high_half(grad_ref[0, :, cols].astype(f32))
        aux = jnp.concatenate([aux_ref[0, 2 * pair], aux_ref[0, 2 * pair + 1]], 0)
        delta = jnp.sum(grad * aux, -1, keepdims=True)
        grad = grad.astype(bf16)
        probs = jnp.exp(product_t(q, kv) + bias - aux[:, :1])
        grad_raw = (probs * (product_t(grad, kv) - delta)).astype(bf16)
        total = total + product_tn(grad_raw, q) + product_tn(probs.astype(bf16), grad)
        gq = join_low(product_n(grad_raw, kv))
        gq_ref[0, :, cols] = (turned(gq, cosine, sine) * HD**-0.5).astype(bf16)
    gkv_ref[...] = total.astype(bf16).reshape(gkv_ref.shape)


def attend_back(q, kv, qpos, qstart, kpos, aux, grad, cosine, sine):
    slots, rows, wide = q.shape
    groups = kv.shape[0]
    heads = wide // HD
    return pl.pallas_call(
        attend_back_kernel,
        out_shape=(
            jax.ShapeDtypeStruct((slots, rows, wide), bf16),
            jax.ShapeDtypeStruct(kv.shape, bf16),
        ),
        grid=(slots,),
        in_specs=attend_specs(slots, groups, rows, wide)
        + [
            pl.BlockSpec((1, heads, rows, LANES), lambda i: (i, 0, 0, 0)),
            pl.BlockSpec((1, rows, wide), lambda i: (i, 0, 0)),
            pl.BlockSpec((rows, LANES), lambda i: (0, 0)),
            pl.BlockSpec((rows, LANES), lambda i: (0, 0)),
        ],
        out_specs=(
            pl.BlockSpec((1, rows, wide), lambda i: (i, 0, 0)),
            pl.BlockSpec((groups, 1, rows, LANES), lambda i: (0, i, 0, 0)),
        ),
        name="attend_back",
    )(q, kv, qpos, qstart, kpos, aux, grad, cosine, sine)


def gather_w_out(w_out):
    groups = lax.axis_size("ctx")
    shards = lax.axis_size("fsdp")
    c = lax.axis_index("ctx")
    f = lax.axis_index("fsdp")
    unit = w_out.shape[0] // groups
    share = jnp.concatenate(gather_z(rows_at(w_out, c * unit, unit))[1:], 0)
    mine = [share] + [swap(share, "ctx", r) for r in range(2, groups, 2)]
    mine = jnp.concatenate(mine, 0)
    theirs = swap(mine, "ctx", 1)
    rank = jnp.arange(1, shards, dtype=jnp.int32) ^ f
    index = jnp.arange(0, groups, 2, dtype=jnp.int32) ^ c
    where = (rank[None, :] * groups + index[:, None]).reshape(-1)
    where_other = (rank[None, :] * groups + (index ^ 1)[:, None]).reshape(-1)
    return place_shares(mine, theirs, w_out, jnp.concatenate([where, where_other]), f, unit)


def place_shares(mine, theirs, own, where, f, unit):
    count = where.shape[0]
    half = count // 2
    extra = own.shape[0] // unit
    cols = own.shape[1]
    where = jnp.concatenate([where, f * extra + jnp.arange(extra, dtype=jnp.int32)])

    def kernel(where_ref, mine_ref, theirs_ref, own_ref, out_ref):
        step = pl.program_id(0)

        @pl.when(step < half)
        def _():
            out_ref[...] = mine_ref[...]

        @pl.when((step >= half) & (step < count))
        def _():
            out_ref[...] = theirs_ref[...]

        @pl.when(step >= count)
        def _():
            out_ref[...] = own_ref[...]

    return pl.pallas_call(
        kernel,
        out_shape=jax.ShapeDtypeStruct(((count + extra) * unit, cols), own.dtype),
        grid_spec=pltpu.PrefetchScalarGridSpec(
            num_scalar_prefetch=1,
            grid=(count + extra,),
            in_specs=[
                pl.BlockSpec((unit, cols), lambda i, w: (jnp.minimum(i, half - 1), 0)),
                pl.BlockSpec((unit, cols), lambda i, w: (jnp.clip(i - half, 0, half - 1), 0)),
                pl.BlockSpec((unit, cols), lambda i, w: (jnp.maximum(i - count, 0), 0)),
            ],
            out_specs=pl.BlockSpec((unit, cols), lambda i, w: (w[i], 0)),
        ),
        name="place_shares",
    )(where, mine, theirs, own)


def on_device(
    hidden_in,
    cotangent,
    doc_ids,
    pair_index,
    w_query,
    w_key,
    w_value,
    w_out,
    w_gate,
    w_up,
    w_down,
    norm_attn,
    norm_ffn,
):
    groups = lax.axis_size("ctx")
    shards = lax.axis_size("fsdp")
    c = lax.axis_index("ctx")
    f = lax.axis_index("fsdp")
    rows = hidden_in.shape[1]
    unit = rows // 2
    width = hidden_in.shape[2]
    copies = max(1, shards // KV)
    twins = [[j * copies + i for i in range(copies)] for j in range(shards // copies)]
    head_cols = w_query.shape[0]
    kv_rows = w_key.shape[0]
    chip_masks = [1 << i for i in range(1, (groups - 1).bit_length())]
    forward_order = [1] + chip_masks
    reverse_order = [1] + chip_masks[::-1]

    slot_ctx = jnp.arange(groups, dtype=jnp.int32) ^ c
    slot_pair = jnp.sum(
        jnp.where(
            slot_ctx[:, None] == jnp.arange(groups, dtype=jnp.int32)[None, :], pair_index[None, :], 0
        ),
        axis=1,
    )
    within = jnp.arange(rows, dtype=jnp.int32)
    block = jnp.where(
        within[None, :] < unit, slot_pair[:, None], 2 * groups - 1 - slot_pair[:, None]
    )
    key_pos = block * unit + within[None, :] % unit
    own_pos = key_pos[0]
    docs = jnp.concatenate([doc_ids] + [swap(doc_ids, "fsdp", r) for r in range(1, shards)], 0)
    own_seg = jnp.concatenate(
        [
            rows_at(docs, slot_pair[0] * unit, unit, 1),
            rows_at(docs, (2 * groups - 1 - slot_pair[0]) * unit, unit, 1),
        ],
        1,
    )
    own_start = jnp.sum((docs[:, None, :] < own_seg[:, :, None]).astype(jnp.int32), -1)
    frequency = jnp.exp(jnp.arange(HD // 2, dtype=f32) * (-2.0 * math.log(10000.0) / HD))
    angles = own_pos.astype(f32)[:, None] * frequency[None, :]
    cosine, sine = jnp.cos(angles), jnp.sin(angles)
    cosine = jnp.concatenate([cosine] * 4, 1)
    sine = jnp.concatenate([-sine, sine] * 2, 1)
    qpos = own_pos[:, None]
    qstart = own_start[:, :, None]
    kpos = key_pos.reshape(1, -1)

    gain_attn = norm_attn.astype(f32)
    gain_ffn = norm_ffn.astype(f32)

    hidden_all = jnp.concatenate(gather_z(hidden_in[0]), 0)
    cot_all = jnp.concatenate(gather_z(cotangent[0]), 0)
    out_full = gather_w_out(w_out)

    if copies > 1:
        key_full = lax.all_gather(w_key, "fsdp", axis=0, tiled=True, axis_index_groups=twins)
        value_full = lax.all_gather(w_value, "fsdp", axis=0, tiled=True, axis_index_groups=twins)
    else:
        key_full, value_full = w_key, w_value
    w_qkv = jnp.concatenate([w_query, key_full, value_full], 0)

    x_all = hidden_all.astype(f32)
    s_all = lax.rsqrt(jnp.mean(x_all * x_all, -1, keepdims=True) + EPSILON)
    normed = (x_all * s_all * gain_attn).astype(bf16)
    qkv = product_t(normed, w_qkv).reshape(shards, rows, -1)
    q, kv_own = rotate(qkv, cosine, sine)
    kv = gather_ctx(kv_own)
    heads_out, aux = attend(q, kv, qpos, qstart, kpos)

    swapped = jnp.concatenate(exchange_z([heads_out[r] for r in range(shards)]), 0)
    mixed = jnp.concatenate([rows_at(swapped, (f ^ j) * rows, rows) for j in range(shards)], 1)
    residual = hidden_in[0].astype(f32) + product_t(mixed, out_full)
    s_ffn = lax.rsqrt(jnp.mean(residual * residual, -1, keepdims=True) + EPSILON)
    normed_ffn = (residual * s_ffn * gain_ffn).astype(bf16)
    nf_all = jnp.concatenate(gather_z(normed_ffn), 0)
    mixed_all = jnp.concatenate(gather_z(mixed), 0)

    gate = product_t(nf_all, w_gate)
    up = product_t(nf_all, w_up)
    grad_units = product_t(cot_all, w_down)
    sig = jax.nn.sigmoid(gate)
    silu = gate * sig
    units = (silu * up).astype(bf16)
    grad_gate = (grad_units * up * sig * (1.0 + gate * (1.0 - sig))).astype(bf16)
    grad_up = (grad_units * silu).astype(bf16)

    grad_w_gate = grad_sum(grad_gate, nf_all, forward_order)
    grad_w_up = grad_sum(grad_up, nf_all, reverse_order)
    part = (product_n(grad_gate, w_gate) + product_n(grad_up, w_up)).astype(bf16)
    g2 = scatter_z(list(part.reshape(shards, rows, width)))
    part = product_n(units, w_down).astype(bf16)
    ffn_out = scatter_z(list(part.reshape(shards, rows, width)))
    half = units.shape[1] // 2
    grad_w_down = jnp.concatenate(
        [
            grad_sum(units[:, :half], cot_all, forward_order),
            grad_sum(units[:, half:], cot_all, reverse_order),
        ],
        0,
    )
    hidden_out = (residual + ffn_out).astype(bf16)

    n_ffn = residual * s_ffn
    grad_gain_ffn = jnp.sum(g2 * n_ffn, 0)
    inner = g2 * gain_ffn
    grad_residual = cotangent[0].astype(f32) + s_ffn * (
        inner - n_ffn * jnp.mean(inner * n_ffn, -1, keepdims=True)
    )
    grad_attn_out = grad_residual.astype(bf16)
    grad_mixed = product_n(grad_attn_out, out_full).astype(bf16)
    grad_heads = jnp.stack(
        exchange_z([rows_at(grad_mixed, (f ^ r) * head_cols, head_cols, 1) for r in range(shards)])
    )
    gq, gkv_terms = attend_back(q, kv, qpos, qstart, kpos, aux, grad_heads, cosine, -sine)
    gkv = sum([t.astype(f32) for t in scatter_ctx(gkv_terms)])
    if copies > 1:
        gkv = lax.psum(gkv, "fsdp", axis_index_groups=twins)
    gkv = gkv.reshape(shards * rows, LANES)
    turn_cos = jnp.tile(cosine[:, :HD], (shards, 1))
    turn_sin = jnp.tile(-sine[:, :HD], (shards, 1))
    gk = gkv[:, :HD]
    flipped = jnp.concatenate([gk[:, HD // 2 :], gk[:, : HD // 2]], 1)
    gk = (gk * turn_cos + flipped * turn_sin).astype(bf16)
    gv = gkv[:, HD:].astype(bf16)
    if copies > 1:
        gk = rows_at(gk, (f % copies) * kv_rows, kv_rows, 1)
        gv = rows_at(gv, (f % copies) * kv_rows, kv_rows, 1)
        w_back = jnp.concatenate([w_query, w_key, w_value], 0)
    else:
        w_back = w_qkv
    grad_qkv = jnp.concatenate([gq.reshape(shards * rows, head_cols), gk, gv], 1)
    g1_part = product_n(grad_qkv, w_back)
    grad_gain_attn = jnp.sum(g1_part * (x_all * s_all), 0)
    g1 = scatter_z(list(g1_part.astype(bf16).reshape(shards, rows, width)))
    grad_w_qkv = grad_sum(grad_qkv, normed, forward_order)

    gao_rows = jnp.concatenate(
        exchange_z([rows_at(grad_attn_out, (f ^ r) * head_cols, head_cols, 1) for r in range(shards)]), 0
    )
    grad_w_out = grad_sum(gao_rows, mixed_all, reverse_order)

    gains = jnp.stack([grad_gain_attn, grad_gain_ffn])
    for mask in forward_order:
        gains = gains + swap(gains, "ctx", mask)
    for mask in [1 << i for i in range((shards - 1).bit_length())]:
        gains = gains + swap(gains, "fsdp", mask)

    x_own = hidden_in[0].astype(f32)
    s_own = lax.rsqrt(jnp.mean(x_own * x_own, -1, keepdims=True) + EPSILON)
    n_own = x_own * s_own
    inner = g1 * gain_attn
    grad_hidden = grad_residual + s_own * (inner - n_own * jnp.mean(inner * n_own, -1, keepdims=True))
    return (
        hidden_out[None],
        grad_hidden.astype(bf16)[None],
        grad_w_qkv[:head_cols],
        grad_w_qkv[head_cols : head_cols + kv_rows],
        grad_w_qkv[head_cols + kv_rows :],
        grad_w_out,
        grad_w_gate,
        grad_w_up,
        grad_w_down,
        gains[0],
        gains[1],
    )


def solution(mesh):
    rows_spec = P("fsdp", "ctx", None)
    shard = P("fsdp", None)
    in_specs = (rows_spec, rows_spec, shard, P()) + (shard,) * 7 + (P(), P())
    out_specs = (rows_spec, rows_spec) + (shard,) * 7 + (P(), P())
    return jax.shard_map(
        on_device, mesh=mesh, in_specs=in_specs, out_specs=out_specs, check_vma=False
    )
```
